32 devices in a mesh: dp: 8 (over z, y), tensor: 4 (over x, core).
Axes of the slice: x: 2, y: 2, z: 4, core: 2. Of those that a mesh axis runs over, the one named last changes fastest.
Arguments:
- block_input: bfloat16 [8192, 768], P(('dp', 'tensor')), may hold values from -64 to 64
- cotangent: bfloat16 [8192, 768], P(('dp', 'tensor')), may hold values from -18 to 18
- lengths: int32 [8], P('dp'), may hold values from 1 to 1024, 5120 in all
- qkv_weight: bfloat16 [3, 768, 768], P(None, 'dp', 'tensor'), may hold values from -0.21875 to 0.21875
- query_bias: bfloat16 [12, 64], P('tensor', 'dp'), may hold values from -3 to 3
- value_bias: bfloat16 [12, 64], P('tensor', 'dp'), may hold values from -0.29882812 to 0.29882812
- out_weight: bfloat16 [768, 768], P('tensor', 'dp'), may hold values from -3.5 to 3.5
- out_bias: float32 [768], P(('dp', 'tensor')), may hold values from -3 to 3
- norm1_gain: float32 [768], P(('dp', 'tensor')), may hold values from 0.5 to 1.5
- norm1_bias: float32 [768], P(('dp', 'tensor')), may hold values from -2 to 2
- up_weight: bfloat16 [768, 3072], P('dp', 'tensor'), may hold values from -0.21875 to 0.21875
- up_bias: bfloat16 [48, 64], P('tensor', 'dp'), may hold values from -3 to 3
- down_weight: bfloat16 [3072, 768], P('tensor', 'dp'), may hold values from -0.109375 to 0.109375
- down_bias: float32 [768], P(('dp', 'tensor')), may hold values from -3 to 3
- norm2_gain: float32 [768], P(('dp', 'tensor')), may hold values from 0.5 to 1.5
- norm2_bias: float32 [768], P(('dp', 'tensor')), may hold values from -2 to 2
Outputs:
- block_output: bfloat16 [8192, 768], P(('dp', 'tensor'))
- input_grad: float32 [8192, 768], P(('dp', 'tensor'))
- qkv_weight_grad: float32 [3, 768, 768], P(None, 'dp', 'tensor')
- query_bias_grad: float32 [12, 64], P('tensor', 'dp')
- value_bias_grad: float32 [12, 64], P('tensor', 'dp')
- out_weight_grad: float32 [768, 768], P('tensor', 'dp')
- out_bias_grad: float32 [768], P(('dp', 'tensor'))
- norm1_gain_grad: float32 [768], P(('dp', 'tensor'))
- norm1_bias_grad: float32 [768], P(('dp', 'tensor'))
- up_weight_grad: float32 [768, 3072], P('dp', 'tensor')
- up_bias_grad: float32 [48, 64], P('tensor', 'dp')
- down_weight_grad: float32 [3072, 768], P('tensor', 'dp')
- down_bias_grad: float32 [768], P(('dp', 'tensor'))
- norm2_gain_grad: float32 [768], P(('dp', 'tensor'))
- norm2_bias_grad: float32 [768], P(('dp', 'tensor'))
The draws below stay inside these ranges and needn't reach their ends.
Inputs may be any that keep to these rules, and one draw needn't show every extreme that they name: lengths[g] positions of slot g are live, counted from its first position; the lengths sum to 5120.
All inputs are finite; a program needn't handle non-finite values. No bound on the sum of `lengths` on one device may be relied on, other than what follows from the above.
Results may differ from the reference program's by a relative error of at most 0.02.
The reference program's roundings to bfloat16 on the way count: a program that leaves them out, or rounds other values in their place, can miss the bound.
Values may be sent and summed in bfloat16 or wider, within the bound.
No kernel may reach another device: no remote copies, remote signals or barrier semaphores. Data moves between devices by JAX's collectives and lax.ppermute only.
A program may use at most 128 MiB of HBM per device.

```python
import math
import jax
import jax.numpy as jnp
import numpy as np
from jax import lax

HEADS = 12
HEAD = 64
D = 768
FF = 3072
SEQ_LEN = 1024
GROUPS = 8
TOKENS = 8192


def draw_block_input(key, part):
    base = jnp.clip(jax.random.normal(key, (TOKENS, D), jnp.float32), -6.0, 6.0)
    return base.astype(jnp.bfloat16)


def draw_cotangent(key, part):
    row_index = jnp.arange(TOKENS, dtype=jnp.int32).astype(jnp.float32)
    growth = 1.0 + 2.0 * row_index / TOKENS
    base = jnp.clip(jax.random.normal(key, (TOKENS, D), jnp.float32), -6.0, 6.0)
    return (base * growth[:, None]).astype(jnp.bfloat16)


def block_levels(key, shape, shards, smallest, largest):
    level, own = 1.0, jax.random.fold_in(key, 6)
    for axis_at, shards_of in shards:
        heights = jnp.exp(jax.random.uniform(jax.random.fold_in(own, axis_at), (shards_of,), jnp.float32, smallest / len(shards), largest / len(shards)))
        level = level * jnp.repeat(heights, shape[axis_at] // shards_of).reshape([-1 if axis == axis_at else 1 for axis in range(len(shape))])
    return level


def length_profile(number_of, total, bound, skew):
    weights = [(1 << 20) // math.isqrt(rank ** skew) + 1 for rank in range(2, number_of + 1)]
    spare, counts = total - bound - (number_of - 1), [1] * (number_of - 1)
    while spare > 0:
        candidates = [i for i in range(number_of - 1) if counts[i] < bound]
        pool, budget = sum([weights[i] for i in candidates]), spare
        for i in candidates:
            more = min(bound - counts[i], max(1, budget * weights[i] // pool), spare)
            counts[i] = counts[i] + more
            spare = spare - more
    return np.array([bound] + counts)


def uneven(stream_key, amount, total, limit, skew):
    if amount == 2:
        one = jax.random.randint(stream_key, (), max(1, total - limit), min(limit, total - 1) + 1)
        return jnp.stack([one, total - one])
    sizes = jnp.asarray(length_profile(amount, total, limit, skew), jnp.int32)
    pairs = (amount - 1) // 2
    giver, taker = sizes[1:1 + 2 * pairs:2], sizes[2:2 + 2 * pairs:2]
    slack = jnp.minimum(giver - 1, limit - taker)
    shifted = jax.random.randint(jax.random.fold_in(stream_key, 1), (pairs,), 0, 1 << 20) % (slack + 1)
    sizes = sizes.at[1:1 + 2 * pairs:2].set(giver - shifted).at[2:2 + 2 * pairs:2].set(taker + shifted)
    return sizes[jax.random.permutation(jax.random.fold_in(stream_key, 2), amount)]


def scatter_about(own_key, shape, scale, bound, split=(), kind=jnp.bfloat16):
    array = jax.random.normal(own_key, shape, jnp.float32) * scale
    if len(split) > 0:
        array = block_levels(own_key, shape, split, -0.22, 0.18) * array
    return jnp.clip(array, min=-bound, max=bound).astype(kind)


def setup_inputs(seed: int = 0) -> dict:
    keys = jax.random.split(jax.random.key(seed), 17)
    block_input = draw_block_input(jax.random.fold_in(keys[16], 71), 0)
    cotangent = draw_cotangent(jax.random.fold_in(keys[16], 71), 0)
    lengths = uneven(keys[2], GROUPS, GROUPS * SEQ_LEN * 5 // 8, SEQ_LEN, 2).astype(jnp.int32)
    qkv_weight = scatter_about(keys[3], (3, D, D), D ** -0.5, 0.21875, ((1, 8), (2, 4)))
    query_bias = scatter_about(keys[4], (HEADS, HEAD), 0.5, 3.0, ((0, 4), (1, 8)))
    value_bias = scatter_about(keys[5], (HEADS, HEAD), 0.05, 0.29882812, ((0, 4), (1, 8)))
    out_weight = scatter_about(keys[6], (D, D), (D // 256) ** -0.5, 3.5, ((0, 4), (1, 8)))
    out_bias = scatter_about(keys[7], (D,), 0.5, 3.0, ((0, 32),), jnp.float32)
    norm1_gain = jnp.clip(1.0 + 0.1 * jax.random.normal(keys[8], (D,), jnp.float32), 0.5, 1.5)
    norm1_bias = scatter_about(keys[9], (D,), 0.3, 2.0, ((0, 32),), jnp.float32)
    up_weight = scatter_about(keys[10], (D, FF), D ** -0.5, 0.21875, ((0, 8), (1, 4)))
    up_bias = scatter_about(keys[11], (FF // HEAD, HEAD), 0.5, 3.0, ((0, 4), (1, 8)))
    down_weight = scatter_about(keys[12], (FF, D), FF ** -0.5, 0.109375, ((0, 4), (1, 8)))
    down_bias = scatter_about(keys[13], (D,), 0.5, 3.0, ((0, 32),), jnp.float32)
    norm2_gain = jnp.clip(1.0 + 0.1 * jax.random.normal(keys[14], (D,), jnp.float32), 0.5, 1.5)
    norm2_bias = scatter_about(keys[15], (D,), 0.3, 2.0, ((0, 32),), jnp.float32)
    return dict(block_input=block_input, cotangent=cotangent, lengths=lengths, qkv_weight=qkv_weight, query_bias=query_bias, value_bias=value_bias, out_weight=out_weight, out_bias=out_bias, norm1_gain=norm1_gain, norm1_bias=norm1_bias, up_weight=up_weight, up_bias=up_bias, down_weight=down_weight, down_bias=down_bias, norm2_gain=norm2_gain, norm2_bias=norm2_bias)


NORM_EPS = 1e-05
NEG_FILL = -1e+30
ROOT_HALF = 0.7071067811865476
INV_ROOT_TAU = 0.3989422804014327

def gelu_pair(pre_act):
    cumul = 0.5 * (1.0 + jax.scipy.special.erf(pre_act * ROOT_HALF))
    density = jnp.exp(-0.5 * pre_act * pre_act) * INV_ROOT_TAU
    return (pre_act * cumul, cumul + pre_act * density)

def layer_norm(summed, gain, shift):
    centre = summed - lax.optimization_barrier(jnp.mean(summed, axis=-1, keepdims=True))
    inverse = lax.rsqrt(lax.optimization_barrier(jnp.mean(centre * centre, axis=-1, keepdims=True)) + NORM_EPS)
    normed = centre * inverse
    return (normed * gain + shift, normed, inverse)

def norm_back(grad_in, normed, inverse, gain):
    scaled = grad_in * gain
    return inverse * (scaled - lax.optimization_barrier(jnp.mean(scaled, axis=-1, keepdims=True)) - normed * lax.optimization_barrier(jnp.mean(scaled * normed, axis=-1, keepdims=True)))

def lowered(values):
    return lax.optimization_barrier(values.astype(jnp.bfloat16))

def reference(block_input, cotangent, lengths, qkv_weight, query_bias, value_bias, out_weight, out_bias, norm1_gain, norm1_bias, up_weight, up_bias, down_weight, down_bias, norm2_gain, norm2_bias):
    wide = jnp.float32
    scale = HEAD ** (-0.5)
    query_w = qkv_weight[0]
    key_w = qkv_weight[1]
    value_w = qkv_weight[2]
    query_b = query_bias.reshape(D).astype(wide)
    value_b = value_bias.reshape(D).astype(wide)
    up_b = up_bias.reshape(FF).astype(wide)

    def split_heads(values):
        return values.astype(wide).reshape(SEQ_LEN, HEADS, HEAD)

    def group_step(carry, item):
        rows, cot_rows, seq_length = item
        live = jnp.arange(SEQ_LEN, dtype=jnp.int32) < seq_length
        queries = lowered(jnp.dot(rows, query_w, preferred_element_type=wide) + query_b)
        key_low = lowered(jnp.dot(rows, key_w, preferred_element_type=wide))
        value_low = lowered(jnp.dot(rows, value_w, preferred_element_type=wide) + value_b)
        query_f = split_heads(queries)
        key_f = split_heads(key_low)
        value_f = split_heads(value_low)
        scores = jnp.einsum('qhd,khd->hqk', query_f, key_f) * scale
        scores = jnp.where(live[None, None, :], scores, NEG_FILL)
        top_score = lax.optimization_barrier(jnp.max(scores, axis=-1, keepdims=True))
        log_total = top_score + jnp.log(lax.optimization_barrier(jnp.sum(jnp.exp(scores - top_score), axis=-1, keepdims=True)))
        prob = jnp.exp(scores - log_total)
        prob_f = lowered(prob).astype(wide)
        heads_out = lowered(jnp.einsum('hqk,khd->qhd', prob_f, value_f).reshape(SEQ_LEN, D))
        summed_one = rows.astype(wide) + jnp.dot(heads_out, out_weight, preferred_element_type=wide) + out_bias
        mixed_one, normed_one, inverse_one = layer_norm(summed_one, norm1_gain, norm1_bias)
        mixed_low = lowered(mixed_one)
        pre_act = jnp.dot(mixed_low, up_weight, preferred_element_type=wide) + up_b
        activated, slope = gelu_pair(pre_act)
        hidden = lowered(activated)
        summed_two = mixed_one + jnp.dot(hidden, down_weight, preferred_element_type=wide) + down_bias
        result_two, normed_two, inverse_two = layer_norm(summed_two, norm2_gain, norm2_bias)
        block_output = result_two.astype(jnp.bfloat16)
        grad_out = cot_rows.astype(wide) * live.astype(wide)[:, None]
        gain_two_grad = lax.optimization_barrier(jnp.sum(grad_out * normed_two, axis=0))
        shift_two_grad = lax.optimization_barrier(jnp.sum(grad_out, axis=0))
        grad_two = norm_back(grad_out, normed_two, inverse_two, norm2_gain)
        down_b_grad = lax.optimization_barrier(jnp.sum(grad_two, axis=0))
        grad_two_low = lowered(grad_two)
        down_grad = jnp.dot(hidden.T, grad_two_low, preferred_element_type=wide)
        grad_pre = jnp.dot(grad_two_low, down_weight.T, preferred_element_type=wide) * slope
        up_b_grad = lax.optimization_barrier(jnp.sum(grad_pre, axis=0))
        grad_pre_low = lowered(grad_pre)
        up_grad = jnp.dot(mixed_low.T, grad_pre_low, preferred_element_type=wide)
        grad_mixed = grad_two + jnp.dot(grad_pre_low, up_weight.T, preferred_element_type=wide)
        gain_one_grad = lax.optimization_barrier(jnp.sum(grad_mixed * normed_one, axis=0))
        shift_one_grad = lax.optimization_barrier(jnp.sum(grad_mixed, axis=0))
        grad_one = norm_back(grad_mixed, normed_one, inverse_one, norm1_gain)
        out_b_grad = lax.optimization_barrier(jnp.sum(grad_one, axis=0))
        grad_one_low = lowered(grad_one)
        out_grad = jnp.dot(heads_out.T, grad_one_low, preferred_element_type=wide)
        grad_heads = split_heads(lowered(jnp.dot(grad_one_low, out_weight.T, preferred_element_type=wide)))
        heads_f = split_heads(heads_out)
        inner = jnp.transpose(lax.optimization_barrier(jnp.sum(grad_heads * heads_f, axis=-1)))
        grad_prob = jnp.einsum('qhd,khd->hqk', grad_heads, value_f)
        grad_score = lowered(prob * (grad_prob - inner[:, :, None])).astype(wide)
        query_grad = jnp.einsum('hqk,khd->qhd', grad_score, key_f) * scale
        key_grad = jnp.einsum('hqk,qhd->khd', grad_score, query_f) * scale
        value_grad = jnp.einsum('hqk,qhd->khd', prob_f, grad_heads)
        query_b_grad = lax.optimization_barrier(jnp.sum(query_grad, axis=0)).reshape(D)
        value_b_grad = lax.optimization_barrier(jnp.sum(value_grad, axis=0)).reshape(D)
        query_low = lowered(query_grad.reshape(SEQ_LEN, D))
        key_low_grad = lowered(key_grad.reshape(SEQ_LEN, D))
        value_low_grad = lowered(value_grad.reshape(SEQ_LEN, D))
        qkv_grad = jnp.stack([jnp.dot(rows.T, query_low, preferred_element_type=wide), jnp.dot(rows.T, key_low_grad, preferred_element_type=wide), jnp.dot(rows.T, value_low_grad, preferred_element_type=wide)])
        input_grad = grad_one + jnp.dot(query_low, query_w.T, preferred_element_type=wide) + jnp.dot(key_low_grad, key_w.T, preferred_element_type=wide) + jnp.dot(value_low_grad, value_w.T, preferred_element_type=wide)
        update = (qkv_grad, query_b_grad, value_b_grad, out_grad, out_b_grad, gain_one_grad, shift_one_grad, up_grad, up_b_grad, down_grad, down_b_grad, gain_two_grad, shift_two_grad)
        carry = tuple((total + piece for total, piece in zip(carry, update)))
        return (carry, (block_output, input_grad))
    zeros_d = jnp.zeros((D,), wide)
    start = (jnp.zeros((3, D, D), wide), zeros_d, zeros_d, jnp.zeros((D, D), wide), zeros_d, zeros_d, zeros_d, jnp.zeros((D, FF), wide), jnp.zeros((FF,), wide), jnp.zeros((FF, D), wide), zeros_d, zeros_d, zeros_d)
    items = (block_input.reshape(GROUPS, SEQ_LEN, D), cotangent.reshape(GROUPS, SEQ_LEN, D), lengths.astype(jnp.int32))
    totals, outputs = lax.scan(group_step, start, items)
    block_output = outputs[0].reshape(TOKENS, D)
    input_grad = outputs[1].reshape(TOKENS, D)
    qkv_grad, query_b_grad, value_b_grad, out_grad, out_b_grad, gain_one_grad, shift_one_grad, up_grad, up_b_grad, down_grad, down_b_grad, gain_two_grad, shift_two_grad = totals
    return (block_output, input_grad, qkv_grad, query_b_grad.reshape(HEADS, HEAD), value_b_grad.reshape(HEADS, HEAD), out_grad, out_b_grad, gain_one_grad, shift_one_grad, up_grad, up_b_grad.reshape(FF // HEAD, HEAD), down_grad, down_b_grad, gain_two_grad, shift_two_grad)
```

```python
import jax
import jax.numpy as jnp
from jax import lax
from jax.sharding import PartitionSpec as P

HEAD = 64
NORM_EPS = 1e-05
NEG_FILL = -1e30
ROOT_HALF = 0.7071067811865476
INV_ROOT_TAU = 0.3989422804014327
WIDE = jnp.float32
NARROW = jnp.bfloat16


def gelu_pair(pre_act):
    cumul = 0.5 * (1.0 + jax.scipy.special.erf(pre_act * ROOT_HALF))
    density = jnp.exp(-0.5 * pre_act * pre_act) * INV_ROOT_TAU
    return (pre_act * cumul, cumul + pre_act * density)


def layer_norm(summed, gain, shift):
    centre = summed - jnp.mean(summed, axis=-1, keepdims=True)
    inverse = lax.rsqrt(jnp.mean(centre * centre, axis=-1, keepdims=True) + NORM_EPS)
    normed = centre * inverse
    return (normed * gain + shift, normed, inverse)


def norm_back(grad_in, normed, inverse, gain):
    scaled = grad_in * gain
    return inverse * (
        scaled
        - jnp.mean(scaled, axis=-1, keepdims=True)
        - normed * jnp.mean(scaled * normed, axis=-1, keepdims=True)
    )


def dot_nn(left, right):
    return jnp.dot(left, right, preferred_element_type=WIDE)


def dot_nt(left, right):
    return lax.dot_general(left, right, (((1,), (1,)), ((), ())), preferred_element_type=WIDE)


def dot_tn(left, right):
    return lax.dot_general(left, right, (((0,), (0,)), ((), ())), preferred_element_type=WIDE)


def stages_of(count):
    bits = count.bit_length() - 1
    stages = []
    stride = 1
    if bits % 2:
        stages.append((1, 2))
        stride = 2
    while stride < count:
        stages.append((stride, 4))
        stride *= 4
    return stages


class Axis:
    def __init__(self, name, size):
        self.name = name
        self.size = size
        self.me = lax.axis_index(name)

    def swap(self, array, mask):
        pairs = [(i, i ^ mask) for i in range(self.size)]
        return lax.ppermute(array, self.name, pairs)

    def digit(self, stride, radix):
        return (self.me // stride) % radix

    def gather_pieces(self, own):
        pieces = {0: own}
        for stride, radix in reversed(stages_of(self.size)):
            keys = list(pieces)
            if len(keys) <= 4:
                for j in range(1, radix):
                    for key in keys:
                        pieces[key ^ (j * stride)] = self.swap(pieces[key], j * stride)
            else:
                stacked = jnp.stack([pieces[key] for key in keys])
                for j in range(1, radix):
                    moved = self.swap(stacked, j * stride)
                    for at, key in enumerate(keys):
                        pieces[key ^ (j * stride)] = moved[at]
        return pieces

    def gather_rows(self, own):
        pieces = self.gather_pieces(own)
        rows = own.shape[0]
        whole = jnp.zeros((self.size * rows,) + own.shape[1:], own.dtype)
        for key, piece in pieces.items():
            first = pl_multiple((self.me ^ key) * rows)
            whole = lax.dynamic_update_slice(whole, piece, (first, 0))
        return whole

    def reorder_small(self, stacked):
        index = jnp.arange(self.size, dtype=jnp.int32)
        chosen = (index[:, None] ^ index[None, :]) == self.me
        return jnp.sum(jnp.where(chosen[:, :, None], stacked[None], 0.0), axis=1)

    def gather_small(self, own):
        stacked = own[None]
        order = [0]
        for stride, radix in reversed(stages_of(self.size)):
            moved = [self.swap(stacked, j * stride) for j in range(1, radix)]
            stacked = jnp.concatenate([stacked] + moved, axis=0)
            order = order + [key ^ (j * stride) for j in range(1, radix) for key in order]
        places = [order.index(k) for k in range(self.size)]
        stacked = jnp.concatenate([stacked[p : p + 1] for p in places], axis=0)
        return self.reorder_small(stacked)

    def scatter_small(self, blocks):
        current = self.reorder_small(blocks)
        for stride, radix in stages_of(self.size):
            current = current.reshape((-1, radix) + current.shape[1:])
            total = current[:, 0]
            for j in range(1, radix):
                total = total + self.swap(current[:, j], j * stride)
            current = total
        return current.reshape(-1)

    def scatter_rows(self, whole):
        rows = whole.shape[0] // self.size
        width = whole.shape[1]
        current = whole
        for stride, radix in stages_of(self.size):
            view = current.reshape(-1, radix, rows, width)
            digit = self.digit(stride, radix)

            def block(j):
                return lax.dynamic_index_in_dim(view, digit ^ j, axis=1, keepdims=False)

            total = block(0).astype(WIDE)
            for j in range(1, radix):
                total = total + self.swap(block(j).astype(NARROW), j * stride).astype(WIDE)
            current = total
        return current.reshape(rows, width)


def pl_multiple(value):
    return value


class Halves:
    def __init__(self, axis):
        self.axis = axis
        self.low = axis.size // 2

    def low_gather(self, own):
        current = own
        bit = self.low // 2
        while bit:
            current = jnp.concatenate([current, self.axis.swap(current, bit)], axis=0)
            bit //= 2
        return current

    def gather(self, own):
        across = self.axis.swap(own, self.low)
        return self.low_gather(own), self.low_gather(across)

    def low_scatter(self, part):
        current = part
        bit = 1
        while bit < self.low:
            half = current.shape[0] // 2
            moved = self.axis.swap(current[half:].astype(NARROW), bit)
            current = current[:half].astype(WIDE) + moved.astype(WIDE)
            bit *= 2
        return current

    def scatter(self, part_a, part_b):
        away = self.low_scatter(part_b)
        far = self.axis.swap(away.astype(NARROW), self.low)
        home = self.low_scatter(part_a)
        return home + far.astype(WIDE)

    def order(self):
        keys = [0]
        bit = self.low // 2
        while bit:
            keys = keys + [k ^ bit for k in keys]
            bit //= 2
        return keys + [k ^ self.low for k in keys]


def local(
    block_input,
    cotangent,
    lengths,
    qkv_weight,
    query_bias,
    value_bias,
    out_weight,
    out_bias,
    norm1_gain,
    norm1_bias,
    up_weight,
    up_bias,
    down_weight,
    down_bias,
    norm2_gain,
    norm2_bias,
    *,
    dp_size,
    tensor_size,
):
    dp = Axis("dp", dp_size)
    tensor = Axis("tensor", tensor_size)
    halves = Halves(tensor)
    scale = HEAD ** (-0.5)
    local_rows, width = block_input.shape
    half_rows = local_rows * tensor_size // 2
    head_width = qkv_weight.shape[2]
    head_count = head_width // HEAD
    slice_width = out_bias.shape[0]

    rows_a, rows_b = halves.gather(block_input)
    packed = jnp.concatenate([qkv_weight[0], qkv_weight[1], qkv_weight[2], out_weight.T], axis=1)
    attn_full = dp.gather_rows(packed)
    vectors = jnp.concatenate([out_bias, norm1_gain, norm1_bias, down_bias, norm2_gain, norm2_bias])
    by_tensor = tensor.gather_small(vectors).reshape(-1)
    column_bias = jnp.concatenate(
        [query_bias.reshape(-1), value_bias.reshape(-1), up_bias.reshape(-1)]
    ).astype(WIDE)
    smalls = dp.gather_small(jnp.concatenate([by_tensor, column_bias]))
    up_full = dp.gather_rows(up_weight)
    down_full = dp.gather_rows(down_weight.T)

    vector_part = smalls[:, : by_tensor.shape[0]].reshape(dp_size, tensor_size, 6, slice_width)
    vector_full = vector_part.transpose(2, 0, 1, 3).reshape(6, width)
    out_vec, gain_one, shift_one, down_vec, gain_two, shift_two = (
        vector_full[i : i + 1] for i in range(6)
    )
    bias_rows = 2 * query_bias.shape[0] + up_bias.shape[0]
    bias_part = smalls[:, by_tensor.shape[0] :].reshape(dp_size, bias_rows, query_bias.shape[1])
    bias_full = bias_part.transpose(1, 0, 2).reshape(bias_rows * HEAD)
    query_full = bias_full[:head_width]
    value_full = bias_full[head_width : 2 * head_width]
    up_bias_full = bias_full[2 * head_width :][None]

    out_full = attn_full[:, 3 * head_width :]
    qkv_full = attn_full[:, : 3 * head_width]

    seq_length = lengths[0]
    bases = jnp.stack([(tensor.me ^ k) * local_rows for k in halves.order()])
    positions = (bases[:, None] + jnp.arange(local_rows, dtype=jnp.int32)[None]).reshape(-1)
    key_mask = (positions < seq_length)[None, :]
    bias_row = jnp.concatenate([query_full, jnp.zeros((head_width,), WIDE), value_full])[None]

    all_rows = jnp.concatenate([rows_a, rows_b], axis=0)
    projected = (dot_nn(all_rows, qkv_full) + bias_row).astype(NARROW)

    def head_of(which, h):
        first = which * head_width + h * HEAD
        return projected[:, first : first + HEAD]

    spans = {"a": slice(0, half_rows), "b": slice(half_rows, 2 * half_rows)}

    def attend(span):
        outs, totals = [], []
        for h in range(head_count):
            scores = dot_nt(head_of(0, h)[span], head_of(1, h)) * scale
            scores = jnp.where(key_mask, scores, NEG_FILL)
            top = jnp.max(scores, axis=-1, keepdims=True)
            log_total = top + jnp.log(jnp.sum(jnp.exp(scores - top), axis=-1, keepdims=True))
            prob_low = jnp.exp(scores - log_total).astype(NARROW)
            outs.append(dot_nn(prob_low, head_of(2, h)).astype(NARROW))
            totals.append(log_total)
        return jnp.concatenate(outs, axis=1), totals

    heads_b, totals_b = attend(spans["b"])
    out_part_b = dot_nt(heads_b, out_full).astype(NARROW)
    heads_a, totals_a = attend(spans["a"])
    out_part_a = dot_nt(heads_a, out_full).astype(NARROW)
    attn_part = halves.scatter(out_part_a, out_part_b)

    summed_one = block_input.astype(WIDE) + attn_part + out_vec
    mixed_one, normed_one, inverse_one = layer_norm(summed_one, gain_one, shift_one)
    mixed_a, mixed_b = halves.gather(mixed_one.astype(NARROW))

    def up_side(mixed):
        pre_act = dot_nn(mixed, up_full) + up_bias_full
        activated, slope = gelu_pair(pre_act)
        hidden = activated.astype(NARROW)
        return hidden, slope, dot_nt(hidden, down_full).astype(NARROW)

    hidden_a, slope_a, mlp_a = up_side(mixed_a)
    hidden_b, slope_b, mlp_b = up_side(mixed_b)
    mlp_part = halves.scatter(mlp_a, mlp_b)

    summed_two = mixed_one + mlp_part + down_vec
    result_two, normed_two, inverse_two = layer_norm(summed_two, gain_two, shift_two)
    block_output = result_two.astype(NARROW)
    row_ids = tensor.me * local_rows + jnp.arange(local_rows, dtype=jnp.int32)
    grad_out = cotangent.astype(WIDE) * (row_ids < seq_length).astype(WIDE)[:, None]
    grad_two = norm_back(grad_out, normed_two, inverse_two, gain_two)
    gain_two_grad = jnp.sum(grad_out * normed_two, axis=0)
    shift_two_grad = jnp.sum(grad_out, axis=0)
    down_vec_grad = jnp.sum(grad_two, axis=0)
    two_a, two_b = halves.gather(grad_two.astype(NARROW))

    def down_side(grad_rows, slope):
        grad_pre = dot_nn(grad_rows, down_full) * slope
        low = grad_pre.astype(NARROW)
        return jnp.sum(grad_pre, axis=0), low, dot_nt(low, up_full).astype(NARROW)

    up_sum_a, pre_a, back_a = down_side(two_a, slope_a)
    up_sum_b, pre_b, back_b = down_side(two_b, slope_b)
    mixed_part = halves.scatter(back_a, back_b)
    down_grad = (dot_tn(two_a, hidden_a) + dot_tn(two_b, hidden_b)).astype(NARROW)
    down_own = dp.scatter_rows(down_grad).T
    up_grad = (dot_tn(mixed_a, pre_a) + dot_tn(mixed_b, pre_b)).astype(NARROW)
    up_own = dp.scatter_rows(up_grad)

    grad_mixed = grad_two + mixed_part
    grad_one = norm_back(grad_mixed, normed_one, inverse_one, gain_one)
    gain_one_grad = jnp.sum(grad_mixed * normed_one, axis=0)
    shift_one_grad = jnp.sum(grad_mixed, axis=0)
    out_vec_grad = jnp.sum(grad_one, axis=0)
    one_a, one_b = halves.gather(grad_one.astype(NARROW))

    vector_grads = jnp.stack(
        [out_vec_grad, gain_one_grad, shift_one_grad, down_vec_grad, gain_two_grad, shift_two_grad]
    ).reshape(6, dp_size, tensor_size, slice_width)
    vector_own = tensor.scatter_small(
        vector_grads.transpose(2, 1, 0, 3).reshape(tensor_size, dp_size * 6 * slice_width)
    ).reshape(dp_size, 6 * slice_width)

    def attend_back(span, grad_rows, heads_out, totals):
        grad_heads = dot_nt_out(grad_rows)
        queries, keys, values = [], [], []
        for h in range(head_count):
            cols = slice(h * HEAD, (h + 1) * HEAD)
            query = head_of(0, h)[span]
            scores = dot_nt(query, head_of(1, h)) * scale
            scores = jnp.where(key_mask, scores, NEG_FILL)
            prob = jnp.exp(scores - totals[h])
            grad_h = grad_heads[:, cols]
            inner = jnp.sum(grad_h.astype(WIDE) * heads_out[:, cols].astype(WIDE), axis=-1, keepdims=True)
            grad_prob = dot_nt(grad_h, head_of(2, h))
            grad_score = (prob * (grad_prob - inner)).astype(NARROW)
            queries.append(dot_nn(grad_score, head_of(1, h)) * scale)
            keys.append(dot_tn(grad_score, query) * scale)
            values.append(dot_tn(prob.astype(NARROW), grad_h))
        return [jnp.concatenate(part, axis=1) for part in (queries, keys, values)]

    def dot_nt_out(grad_rows):
        return dot_nn(grad_rows, out_full).astype(NARROW)

    query_a, key_a, value_a = attend_back(spans["a"], one_a, heads_a, totals_a)
    query_b, key_b, value_b = attend_back(spans["b"], one_b, heads_b, totals_b)
    key_grad = key_a + key_b
    value_grad = value_a + value_b
    query_sum = jnp.sum(query_a, axis=0) + jnp.sum(query_b, axis=0)
    value_sum = jnp.sum(value_grad, axis=0)
    query_grad = jnp.concatenate([query_a, query_b], axis=0)
    projected_grad = jnp.concatenate([query_grad, key_grad, value_grad], axis=1).astype(NARROW)

    out_grad = (dot_tn(one_a, heads_a) + dot_tn(one_b, heads_b)).astype(NARROW)
    out_own = dp.scatter_rows(out_grad).T
    qkv_grad = dot_tn(all_rows, projected_grad).astype(NARROW)
    qkv_own = dp.scatter_rows(qkv_grad)
    input_b = dot_nt(projected_grad[spans["b"]], qkv_full).astype(NARROW)
    input_a = dot_nt(projected_grad[spans["a"]], qkv_full).astype(NARROW)
    input_grad = grad_one + halves.scatter(input_a, input_b)

    bias_grads = jnp.concatenate([query_sum, value_sum, up_sum_a + up_sum_b])
    bias_blocks = bias_grads.reshape(bias_rows, dp_size, query_bias.shape[1]).transpose(1, 0, 2)
    small_own = dp.scatter_small(
        jnp.concatenate([vector_own, bias_blocks.reshape(dp_size, -1)], axis=1)
    )
    vec = small_own[: 6 * slice_width].reshape(6, slice_width)
    bias = small_own[6 * slice_width :].reshape(bias_rows, query_bias.shape[1])
    heads = query_bias.shape[0]
    qkv_out = jnp.stack([qkv_own[:, c * head_width : (c + 1) * head_width] for c in range(3)])
    return (
        block_output,
        input_grad,
        qkv_out,
        bias[:heads],
        bias[heads : 2 * heads],
        out_own,
        vec[0],
        vec[1],
        vec[2],
        up_own,
        bias[2 * heads :],
        down_own,
        vec[3],
        vec[4],
        vec[5],
    )


def solution(mesh):
    rows = P(("dp", "tensor"), None)
    vector = P(("dp", "tensor"))
    crossed = P("tensor", "dp")

    def body(*arrays):
        return local(*arrays, dp_size=mesh.shape["dp"], tensor_size=mesh.shape["tensor"])

    qkv = P(None, "dp", "tensor")
    return jax.shard_map(
        body,
        mesh=mesh,
        in_specs=(
            rows, rows, P("dp"), qkv, crossed, crossed, crossed, vector, vector, vector,
            P("dp", "tensor"), crossed, crossed, vector, vector, vector,
        ),
        out_specs=(
            rows, rows, qkv, crossed, crossed, crossed, vector, vector, vector,
            P("dp", "tensor"), crossed, crossed, vector, vector, vector,
        ),
        check_vma=False,
    )
```
